256 devices in a mesh: req: 64 (over z, y, core), tp: 4 (over x).
Axes of the slice: x: 4, y: 4, z: 8, core: 2. Of those that a mesh axis runs over, the one named last changes fastest.
Arguments:
- drafts: bfloat16 [128, 64, 1536], P('req'), may hold values from -27 to 27, as said below
- gain_attn: float32 [1536], replicated, may hold values from 0.1 to 1.9
- w_query: bfloat16 [1536, 1536], P(None, 'tp'), may hold values from -0.15625 to 0.15625
- key_value_weight: bfloat16 [1536, 512], replicated, may hold values from -0.15625 to 0.15625
- w_output: bfloat16 [1536, 1536], P('tp'), may hold values from -0.5 to 0.5
- cache: bfloat16 [128, 2, 2, 3072, 128], P('req'), may hold values from -130 to 130, as said below
- lengths: int32 [128], P('req'), may hold values from 1 to 3072, 131072 in all
- tree_mask: int32 [128, 64, 64], P('req'), may hold values from 0 to 1, as said below
- depths: int32 [128, 64], P('req'), may hold values from 0 to 63, as said below
- gain_moe: float32 [1536], replicated, may hold values from 0.1 to 1.9
- w_router: bfloat16 [1536, 32], replicated, may hold values from -0.15625 to 0.15625
- expert_ids: int32 [128, 64, 4], P('req'), may hold values from 0 to 31, all different within a row; in each aligned block of 128 rows (0 to 127, 128 to 255, ..., all dimensions but the last counted through in order) at most 32 rows name the same one
- w_in: bfloat16 [64, 1536, 2, 384], P('req'), may hold values from -0.15625 to 0.15625
- w_out: bfloat16 [64, 384, 1536], P('req'), may hold values from -0.21875 to 0.21875
- slots: int32 [128, 64], P('req'), may hold values from -1 to 15, as said below
- order: int32 [128], P('req'), may hold values from 0 to 127, each once
Outputs:
- tree_out: bfloat16 [128, 64, 1536], P('req', None, 'tp')
- accepted: bfloat16 [128, 16, 1536], P('req', None, 'tp')
The draws below stay inside these ranges and needn't reach their ends.
Inputs may be any that keep to these rules, and one draw needn't show every extreme that they name: `drafts`: values lie within this range. `cache`: values lie within this range. `tree_mask`: each request's tokens form a tree rooted at token 0, the parent of token t being one of tokens t - 4 to t - 1; entry [s, i, j] is 1 exactly when j is i or an ancestor of i. `depths`: depth of each token in its tree, agreeing with tree_mask; the root has depth 0. In every draw some request's tree is a single chain. In each request the tokens on the path from the root to one token of depth d carry slots 0 to d (their depths), with d + 1 <= 16; all other tokens carry -1. In every draw some request fills all 16 slots. `expert_ids`: each token names 4 different experts; among the tokens of one device no expert is named by more than 32 tokens. `order`: each request is served in exactly one serving slot.
All inputs are finite; a program needn't handle non-finite values. No bound on the sum of `lengths` on one device may be relied on, other than what follows from the above.
Results may differ from the reference program's by a relative error of at most 0.011.
Values may be sent and summed in bfloat16 or wider, within the bound.
A program may use at most 64 MiB of HBM per device.

```python
import math
import jax
import jax.numpy as jnp
import numpy as np
from jax import lax

MODEL_WIDTH = 1536
QUERY_HEADS = 12
KEY_VALUE_HEADS = 2
HEAD_SIZE = 128
EXPERTS = 32
FF = 768
TOPK = 4
TREE = 64
KEEP = 16
REQ_DEV = 2
CACHE_LONGEST = 3072
REQUEST_TOTAL = 128
CAP = 32
N_REQ = 64


def draw_drafts(key, part):
    key_a, random_key_second, random_key_third = jax.random.split(jax.random.fold_in(key, 3), 3)
    row_scale = jnp.exp(jax.random.uniform(key_a, (REQUEST_TOTAL, TREE, 1), jnp.float32, jnp.log(0.3), jnp.log(3.0)))
    col_scale = jnp.exp(jax.random.uniform(random_key_second, (MODEL_WIDTH,), jnp.float32, jnp.log(0.3), jnp.log(3.0)))
    noise = jnp.clip(jax.random.normal(random_key_third, (REQUEST_TOTAL, TREE, MODEL_WIDTH), jnp.float32), -3.0, 3.0)
    return (noise * row_scale * col_scale).astype(jnp.bfloat16)


def draw_cache(key, part):
    key_a = jax.random.fold_in(jax.random.fold_in(key, 5), 0)
    array_shape = (REQUEST_TOTAL, 2, KEY_VALUE_HEADS, CACHE_LONGEST, HEAD_SIZE)
    values = jnp.clip(jax.random.normal(key_a, array_shape, jnp.float32), -4.0, 4.0)
    return values.astype(jnp.bfloat16)


def tree_parts(key):
    key_a, random_key_second, random_key_third, key_d = jax.random.split(jax.random.fold_in(key, 11), 4)
    index = jnp.arange(TREE, dtype=jnp.int32)
    row_ids = jnp.arange(REQUEST_TOTAL, dtype=jnp.int32)
    forced = jax.random.randint(random_key_third, (), 0, REQUEST_TOTAL)
    lowest = jnp.maximum(index - 4, 0)
    span = jnp.maximum(index - lowest, 1)
    parent = lowest[None, :] + jax.random.randint(key_a, (REQUEST_TOTAL, TREE), 0, 1 << 20) % span[None, :]
    chain = jnp.maximum(index - 1, 0)
    parent = jnp.where((row_ids == forced)[:, None], chain[None, :], parent)
    depth0 = jnp.zeros((REQUEST_TOTAL, TREE), jnp.int32)
    ancest0 = jnp.zeros((REQUEST_TOTAL, TREE, TREE), jnp.int32).at[:, 0, 0].set(1)

    def grow(node, carry):
        depth, ancest = carry
        parents = parent[:, node]
        new_depth = depth[row_ids, parents] + 1
        new_row = jnp.maximum(ancest[row_ids, parents], (index == node).astype(jnp.int32)[None, :])
        return (depth.at[:, node].set(new_depth), ancest.at[:, node].set(new_row))
    depth, ancest = lax.fori_loop(1, TREE, grow, (depth0, ancest0))
    target = jax.random.randint(random_key_second, (REQUEST_TOTAL,), KEEP // 2, KEEP)
    target = jnp.where(row_ids == forced, KEEP - 1, target)
    score = jnp.where(depth == target[:, None], jax.random.randint(key_d, (REQUEST_TOTAL, TREE), 0, 1 << 16) * TREE + index[None, :] + 1, 0)
    leaf = jnp.argmax(score, axis=1)
    on_path = ancest[row_ids, leaf]
    slot_vals = jnp.where(on_path > 0, depth, -1)
    return (ancest, depth, slot_vals)


def draw_tree_mask(key, part):
    return tree_parts(key)[0]


def draw_depths(key, part):
    return tree_parts(key)[1]


def draw_slots(key, part):
    return tree_parts(key)[2]


def level_of(stream_key, dims, shards, least, largest):
    def one(position, parts):
        heights = jax.random.uniform(jax.random.fold_in(jax.random.fold_in(stream_key, 6), position), (parts,), jnp.float32, least / len(shards), largest / len(shards))
        return jnp.repeat(jnp.exp(heights), dims[position] // parts).reshape((-1,) + (1,) * (len(dims) - position - 1))

    factor_of = one(*shards[0])
    for cut in shards[1:]:
        factor_of = factor_of * one(*cut)
    return factor_of


def length_profile(number_of, total, reach, slope):
    weights = [(1 << 20) // math.isqrt(grade ** slope) + 1 for grade in range(2, number_of + 1)]
    surplus, holding = total - reach - (number_of - 1), [1] * (number_of - 1)
    while surplus > 0:
        movable = [i for i in range(number_of - 1) if holding[i] < reach]
        mass, left = sum([weights[i] for i in movable]), surplus
        for i in movable:
            more = min(reach - holding[i], max(1, left * weights[i] // mass), surplus)
            holding[i] = holding[i] + more
            surplus = surplus - more
    return np.array([reach] + holding)


def uneven(stream_key, amount, total, bound, lean):
    if amount == 2:
        one = jax.random.randint(stream_key, (), max(1, total - bound), min(bound, total - 1) + 1)
        return jnp.stack([one, total - one])
    tallies = jnp.asarray(length_profile(amount, total, bound, lean), jnp.int32)
    couples = (amount - 1) // 2
    donor, taker = tallies[1:1 + 2 * couples:2], tallies[2:2 + 2 * couples:2]
    margin = jnp.minimum(donor - 1, bound - taker)
    passed = jax.random.randint(jax.random.fold_in(stream_key, 1), (couples,), 0, 1 << 20) % (margin + 1)
    tallies = tallies.at[1:1 + 2 * couples:2].set(donor - passed).at[2:2 + 2 * couples:2].set(taker + passed)
    return tallies[jax.random.permutation(jax.random.fold_in(stream_key, 2), amount)]


def routed_block(own_key, own, number, rows, count, top, reach, slope):
    order = jax.random.permutation(own_key, count)
    crowded, usual = shares(count, rows * top, reach, slope, True), shares(count, rows * top, reach, slope, False)
    places = jnp.arange(count)

    def named(tallies, turn):
        used = int((tallies > 0).sum())
        fixed = max(1, used // 4)
        shifted = fixed + (places - fixed + turn * (used - fixed)) % max(1, count - fixed)
        return jnp.zeros((count,), jnp.int32).at[order[jnp.where(places < fixed, places, shifted)]].set(jnp.asarray(tallies, jnp.int32))

    tallies = jnp.where(number % 4 == 0, named(crowded, number // 4), named(usual, number - number // 4 - 1))
    mixed = jax.random.permutation(jax.random.fold_in(own, 3), count)
    donor, receiver = mixed[0:count // 2 * 2:2], mixed[1:count // 2 * 2:2]
    room = jnp.minimum(tallies[donor] - 1, reach - tallies[receiver]) // 2
    room = jnp.where((donor == order[0]) | (receiver == order[0]) | (tallies[receiver] == 0), 0, jnp.maximum(room, 0))
    shifted = jax.random.randint(jax.random.fold_in(own, 4), (count // 2,), 0, 1 << 20) % (room + 1)
    tallies = tallies.at[donor].add(-shifted).at[receiver].add(shifted)
    items = jnp.searchsorted(jnp.cumsum(tallies), jnp.arange(rows * top), side="right").astype(jnp.int32)
    table = items.reshape(top, rows).T
    table = table[jax.random.permutation(jax.random.fold_in(own, 1), rows)]
    turn = jax.random.randint(jax.random.fold_in(own, 2), (rows, 1), 0, top)
    return jnp.take_along_axis(table, (jnp.arange(top)[None, :] + turn) % top, axis=1)


def shares(amount, total, most, slope, full):
    portions = [(1 << 20) // math.isqrt(standing ** slope) + 1 for standing in range(1, amount + 1)]
    largest = most if full else min(most, max(-(-total // amount), total * portions[0] // sum(portions)))
    least = 1 if total - largest >= amount - 1 else 0
    holding, spare = [largest] + [least] * (amount - 1), total - largest - least * (amount - 1)
    while spare > 0:
        free = [i for i in range(1, amount) if holding[i] < largest] or [i for i in range(1, amount) if holding[i] < most]
        pool, budget = sum([portions[i] for i in free]), spare
        for i in free:
            addition = min(most - holding[i], max(1, budget * portions[i] // pool), spare)
            holding[i] = holding[i] + addition
            spare = spare - addition
    return np.array(holding)


def normal_values(rng, dims, deviation, most, cuts=(), kind=jnp.bfloat16):
    drawn = deviation * jax.random.normal(rng, dims, jnp.float32)
    if cuts:
        drawn = drawn * level_of(rng, dims, cuts, -0.22, 0.18)
    return jnp.clip(drawn, -most, most).astype(kind)


def setup_inputs(seed: int = 0) -> dict:
    streams_of = jax.random.split(jax.random.key(seed), 17)
    drafts = draw_drafts(jax.random.fold_in(streams_of[16], 71), 0)
    gain_attn = jnp.clip(1.0 + 0.18 * jax.random.normal(streams_of[1], (MODEL_WIDTH,), jnp.float32), 0.1, 1.9)
    w_query = normal_values(streams_of[2], (MODEL_WIDTH, QUERY_HEADS * HEAD_SIZE), MODEL_WIDTH ** -0.5, 0.15625, ((1, 4),))
    key_value_weight = normal_values(streams_of[3], (MODEL_WIDTH, 2 * KEY_VALUE_HEADS * HEAD_SIZE), MODEL_WIDTH ** -0.5, 0.15625)
    w_output = normal_values(streams_of[4], (QUERY_HEADS * HEAD_SIZE, MODEL_WIDTH), HEAD_SIZE ** -0.5, 0.5, ((0, 4),))
    cache = draw_cache(jax.random.fold_in(streams_of[16], 71), 0)
    lengths = uneven(streams_of[6], REQUEST_TOTAL, REQUEST_TOTAL * CACHE_LONGEST // 3, CACHE_LONGEST, 2).astype(jnp.int32)
    tree_mask = draw_tree_mask(jax.random.fold_in(streams_of[16], 71), 0)
    depths = draw_depths(jax.random.fold_in(streams_of[16], 71), 0)
    gain_moe = jnp.clip(1.0 + 0.18 * jax.random.normal(streams_of[9], (MODEL_WIDTH,), jnp.float32), 0.1, 1.9)
    w_router = normal_values(streams_of[10], (MODEL_WIDTH, EXPERTS), MODEL_WIDTH ** -0.5, 0.15625)
    expert_ids_keys = jax.random.split(jax.random.fold_in(streams_of[11], 1), REQUEST_TOTAL * TREE // (REQ_DEV * TREE))
    expert_ids_turns = jax.random.permutation(jax.random.fold_in(streams_of[11], 3), REQUEST_TOTAL * TREE // (REQ_DEV * TREE))
    expert_ids = jax.vmap(lambda own, number: routed_block(jax.random.fold_in(streams_of[11], 2), own, number, REQ_DEV * TREE, EXPERTS, TOPK, CAP, 2))(expert_ids_keys, expert_ids_turns).reshape((REQUEST_TOTAL, TREE, TOPK))
    w_in = normal_values(streams_of[12], (2 * EXPERTS, MODEL_WIDTH, 2, FF // 2), MODEL_WIDTH ** -0.5, 0.15625, ((0, 64),))
    w_out = normal_values(streams_of[13], (2 * EXPERTS, FF // 2, MODEL_WIDTH), FF ** -0.5, 0.21875, ((0, 64),))
    slots = draw_slots(jax.random.fold_in(streams_of[16], 71), 0)
    order = jax.random.permutation(streams_of[15], REQUEST_TOTAL).astype(jnp.int32)
    return {"drafts": drafts, "gain_attn": gain_attn, "w_query": w_query, "key_value_weight": key_value_weight, "w_output": w_output, "cache": cache, "lengths": lengths, "tree_mask": tree_mask, "depths": depths, "gain_moe": gain_moe, "w_router": w_router, "expert_ids": expert_ids, "w_in": w_in, "w_out": w_out, "slots": slots, "order": order}


EPSILON = 1e-06
THETA = 1000000.0

def rms_norm(values, gain_vec):
    return values * lax.rsqrt(lax.optimization_barrier(jnp.mean(values * values, axis=-1, keepdims=True)) + EPSILON) * gain_vec

def rotary(values, positions):
    half_dim = values.shape[-1] // 2
    freqs = jnp.exp(-jnp.log(THETA) * jnp.arange(half_dim, dtype=jnp.float32) / half_dim)
    angles = positions.astype(jnp.float32)[..., None] * freqs
    cosine = jnp.cos(angles)
    sine = jnp.sin(angles)
    first = values[..., :half_dim]
    second = values[..., half_dim:]
    return jnp.concatenate([first * cosine - second * sine, second * cosine + first * sine], axis=-1)

def reference(drafts, gain_attn, w_query, key_value_weight, w_output, cache, lengths, tree_mask, depths, gain_moe, w_router, expert_ids, w_in, w_out, slots, order):
    request_list, draft_tree, width = drafts.shape
    cache_len = cache.shape[3]
    head_group = QUERY_HEADS // KEY_VALUE_HEADS
    scale = HEAD_SIZE ** (-0.5)
    inputs = drafts.astype(jnp.float32).reshape(request_list * draft_tree, width)
    normalized_input = rms_norm(inputs, gain_attn).astype(jnp.bfloat16)
    positions = lengths[:, None] + depths
    query_all = jnp.dot(normalized_input, w_query, preferred_element_type=jnp.float32).reshape(request_list, draft_tree, QUERY_HEADS, HEAD_SIZE)
    key_value = jnp.dot(normalized_input, key_value_weight, preferred_element_type=jnp.float32).reshape(request_list, draft_tree, 2, KEY_VALUE_HEADS, HEAD_SIZE)
    query_all = rotary(query_all, positions[:, :, None]).astype(jnp.bfloat16)
    key_new = rotary(key_value[:, :, 0], positions[:, :, None]).astype(jnp.bfloat16)
    val_new = key_value[:, :, 1].astype(jnp.bfloat16)

    def attend(pack):
        query_request, k_req, v_req, c_req, limit, allowed = pack
        query_heads_rows = query_request.astype(jnp.float32).reshape(draft_tree, KEY_VALUE_HEADS, head_group, HEAD_SIZE)
        cache_scores = jnp.einsum('tkgd,kcd->kgtc', query_heads_rows, c_req[0].astype(jnp.float32)) * scale
        tree_scores = jnp.einsum('tkgd,skd->kgts', query_heads_rows, k_req.astype(jnp.float32)) * scale
        inside = jnp.arange(cache_len) < limit
        cache_scores = jnp.where(inside[None, None, None, :], cache_scores, -jnp.inf)
        tree_scores = jnp.where((allowed > 0)[None, None], tree_scores, -jnp.inf)
        peak = jnp.maximum(lax.optimization_barrier(jnp.max(cache_scores, axis=-1)), lax.optimization_barrier(jnp.max(tree_scores, axis=-1)))
        cache_w = jnp.exp(cache_scores - peak[..., None])
        tree_w = jnp.exp(tree_scores - peak[..., None])
        totals = lax.optimization_barrier(jnp.sum(cache_w, axis=-1)) + lax.optimization_barrier(jnp.sum(tree_w, axis=-1))
        cache_p = cache_w.astype(jnp.bfloat16).astype(jnp.float32)
        tree_p = tree_w.astype(jnp.bfloat16).astype(jnp.float32)
        mixed = jnp.einsum('kgtc,kcd->kgtd', cache_p, c_req[1].astype(jnp.float32))
        mixed = mixed + jnp.einsum('kgts,skd->kgtd', tree_p, v_req.astype(jnp.float32))
        mixed = mixed / totals[..., None]
        return mixed.transpose(2, 0, 1, 3).reshape(draft_tree, QUERY_HEADS * HEAD_SIZE).astype(jnp.bfloat16)
    heads = lax.map(attend, (query_all, key_new, val_new, cache, lengths, tree_mask))
    attn = jnp.dot(heads.reshape(request_list * draft_tree, QUERY_HEADS * HEAD_SIZE), w_output, preferred_element_type=jnp.float32)
    resid = inputs + attn
    normed2 = rms_norm(resid, gain_moe).astype(jnp.bfloat16)
    logits = jnp.dot(normed2, w_router, preferred_element_type=jnp.float32)
    ids = expert_ids.reshape(request_list * draft_tree, TOPK)
    chosen = jax.nn.sigmoid(jnp.take_along_axis(logits, ids, axis=1))
    gates = (chosen / lax.optimization_barrier(jnp.sum(chosen, axis=1, keepdims=True))).astype(jnp.bfloat16)
    half_ff = FF // 2
    gate_up = w_in.reshape(EXPERTS, 2, width, 2, half_ff).transpose(0, 2, 3, 1, 4).reshape(EXPERTS, width, 2, FF)
    down = w_out.reshape(EXPERTS, FF, width)
    most_rows = N_REQ * CAP

    def expert_step(carry, expert):
        hits = jnp.any(ids == expert, axis=1)
        picked = jnp.nonzero(hits, size=most_rows, fill_value=0)[0]
        valid = jnp.arange(most_rows) < jnp.sum(hits.astype(jnp.int32))
        rows_in = normed2[picked]
        weights_in = lax.dynamic_index_in_dim(gate_up, expert, 0, keepdims=False)
        weights_down = lax.dynamic_index_in_dim(down, expert, 0, keepdims=False)
        gate = jnp.dot(rows_in, weights_in[:, 0], preferred_element_type=jnp.float32)
        upper = jnp.dot(rows_in, weights_in[:, 1], preferred_element_type=jnp.float32)
        act = (jax.nn.relu(gate) * upper).astype(jnp.bfloat16)
        output = jnp.zeros((most_rows, width), jnp.float32)
        for half_index in range(2):
            piece_out = jnp.dot(act[:, half_index * half_ff:(half_index + 1) * half_ff], weights_down[half_index * half_ff:(half_index + 1) * half_ff], preferred_element_type=jnp.float32)
            rounded = lax.optimization_barrier(piece_out.astype(jnp.bfloat16))
            output = output + rounded.astype(jnp.float32)
        token_gate = lax.optimization_barrier(jnp.sum(jnp.where(ids == expert, gates.astype(jnp.float32), 0.0), axis=1))
        row_gate = jnp.where(valid, token_gate[picked], 0.0)
        return (carry.at[picked].add(row_gate[:, None] * output), None)
    mixture, unused = lax.scan(expert_step, jnp.zeros((request_list * draft_tree, width), jnp.float32), jnp.arange(EXPERTS).astype(jnp.int32))
    tree_out = (resid + mixture).astype(jnp.bfloat16).reshape(request_list, draft_tree, width)
    dest_req = jnp.broadcast_to(order[:, None], slots.shape)
    dest_slot = jnp.where(slots >= 0, slots, KEEP)
    accepted = jnp.zeros((request_list, KEEP, width), jnp.bfloat16).at[dest_req, dest_slot].set(tree_out, mode='drop')
    return (tree_out, accepted)
```

```python
import jax
import jax.numpy as jnp
from jax import lax
from jax.experimental import pallas as pl
from jax.experimental.pallas import tpu as pltpu
from jax.sharding import PartitionSpec as P

KEEP = 16
EPSILON = 1e-06
THETA = 1000000.0
NX = 4
NY = 4
NZ = 8
CHIPS = 32
SHARE = 8
HEAD = 128
HEADS = 3
TREE = 64
TOKENS = 128
WIDTH = 1536
QUARTER = 384
LONGEST = 3072
BLOCK = 512
HALF_FF = 384
PEERS = 38
BATCHES = ((0, 4), (1, 7), (2, 6), (3, 5))
SEND_ORDER = (1, 7, 2, 6, 3, 5, 4, 0)
F32 = jnp.float32
BF16 = jnp.bfloat16
MESH = pl.DeviceIdType.MESH


def mm(left, right):
    return jnp.dot(left, right, preferred_element_type=F32)


def mm_nt(left, right):
    return lax.dot_general(left, right, (((1,), (1,)), ((), ())), preferred_element_type=F32)


def mm_tn(left, right):
    return lax.dot_general(left, right, (((0,), (0,)), ((), ())), preferred_element_type=F32)


def iota(shape, dim):
    return lax.broadcasted_iota(jnp.int32, shape, dim)


def to_rows(blocks):
    shape = blocks.shape
    rows = 1
    for size in shape[:-1]:
        rows *= size
    return blocks.astype(F32).reshape(rows, shape[-1]).astype(BF16)


def wait_for(ref, sem):
    pltpu.make_async_copy(ref, ref, sem).wait()


def layer(
    drafts_h,
    gain_attn_h,
    w_query_h,
    kv_weight_h,
    w_output_h,
    cache_h,
    lengths_s,
    tree_mask_h,
    depths_h,
    gain_moe_h,
    w_router_h,
    ids_h,
    w_in_h,
    w_out_h,
    slots_h,
    order_s,
    tree_out_ref,
    accepted_ref,
    drafts,
    gain_attn,
    w_qkv,
    w_output,
    kbuf,
    vbuf,
    tree_mask,
    depths,
    gain_moe,
    w_router,
    ids,
    w_in_raw,
    w_in,
    w_out,
    slots,
    load_sem,
    rs_send,
    rs_recv,
    rs_ssem,
    rs_rsem,
    ag_all,
    ag_ssem,
    ag_rsem,
    dmat,
    comb,
    normed2,
    send_buf,
    rows,
    own_part,
    sib_send,
    sib_recv,
    ret_send,
    ret,
    disp_ssem,
    disp_rsem,
    relay_ssem,
    relay_rsem,
    sib_ssem,
    sib_rsem,
    ret_ssem,
    ret_rsem,
    mix_send,
    mix_recv,
    mix_ssem,
    mix_rsem,
    ord_all,
    ord_ssem,
    ord_rsem,
    z_all,
    z_ssem,
    z_rsem,
    yc_send,
    yc_recv,
    yc_ssem,
    yc_rsem,
):
    x = lax.axis_index("tp")
    req = lax.axis_index("req")
    core = req % 2
    chip = req // 2
    y = chip % NY
    z = chip // NY
    kv_head = x // 2
    other = 1 - core

    def place(zz, yy, cc):
        return ((zz * NY + yy) * 2 + cc, x)

    barrier = pltpu.get_barrier_semaphore()

    def greet(device):
        pl.semaphore_signal(barrier, inc=1, device_id=device, device_id_type=MESH)

    for dx in range(1, NX):
        greet((req, (x + dx) % NX))
    for dz in range(NZ):
        for dy in range(NY):
            if dz or dy:
                greet(place((z + dz) % NZ, (y + dy) % NY, core))
    for dy in range(NY):
        greet(place(z, (y + dy) % NY, other))

    loads = []

    def load(source, target):
        copy = pltpu.make_async_copy(source, target, load_sem.at[len(loads)])
        copy.start()
        loads.append(copy)
        return copy

    l_drafts = load(drafts_h, drafts)
    l_gain = load(gain_attn_h, gain_attn)
    l_depths = load(depths_h, depths)
    l_wq = load(w_query_h, w_qkv.at[:, pl.ds(0, QUARTER)])
    l_wk = load(
        kv_weight_h.at[:, pl.ds(pl.multiple_of(kv_head * HEAD, HEAD), HEAD)],
        w_qkv.at[:, pl.ds(QUARTER, HEAD)],
    )
    l_wv = load(
        kv_weight_h.at[:, pl.ds(pl.multiple_of(256 + kv_head * HEAD, HEAD), HEAD)],
        w_qkv.at[:, pl.ds(QUARTER + HEAD, HEAD)],
    )
    l_mask = load(tree_mask_h, tree_mask)
    l_cache = []
    for request in range(2):
        l_cache.append(load(cache_h.at[request, 0, kv_head], kbuf.at[request]))
        l_cache.append(load(cache_h.at[request, 1, kv_head], vbuf.at[request]))
    l_wo = load(w_output_h, w_output)
    l_ids = load(ids_h, ids)
    l_win = load(w_in_h, w_in_raw)
    l_gain2 = load(gain_moe_h, gain_moe)
    l_router = load(w_router_h, w_router)
    l_slots = load(slots_h, slots)
    l_wout = load(w_out_h, w_out)

    l_depths.wait()
    length0 = lengths_s[0]
    length1 = lengths_s[1]
    row = iota((TOKENS, TOKENS), 0)
    col = iota((TOKENS, TOKENS), 1)
    spread = jnp.concatenate([depths[...], depths[...]], axis=1)
    pos_lane = jnp.where(
        iota((1, TOKENS), 1) < TREE, spread[0:1, :] + length0, spread[1:2, :] + length1
    ).astype(F32)
    positions = jnp.sum(jnp.where(row == col, pos_lane, 0.0), axis=1, keepdims=True)
    lane = iota((1, HEAD), 1) % (HEAD // 2)
    freqs = jnp.exp(-jnp.log(jnp.float32(THETA)) * lane.astype(F32) / (HEAD // 2))
    angles = positions * freqs
    cosine = jnp.cos(angles)
    sine = jnp.sin(angles)
    sine = jnp.where(col < HEAD // 2, -sine, sine)

    def rotary(values):
        return values * cosine + pltpu.roll(values, HEAD // 2, 1) * sine

    l_drafts.wait()
    l_gain.wait()
    inputs = drafts[...].reshape(TOKENS, WIDTH).astype(F32)
    mean = jnp.mean(inputs * inputs, axis=-1, keepdims=True)
    normed = (inputs * lax.rsqrt(mean + EPSILON) * gain_attn[...]).astype(BF16)
    l_wq.wait()
    l_wk.wait()
    l_wv.wait()
    qkv = mm(normed, w_qkv[...])
    heads_q = [
        rotary(qkv[:, h * HEAD : (h + 1) * HEAD]).astype(BF16) for h in range(HEADS)
    ]
    key_new = rotary(qkv[:, QUARTER : QUARTER + HEAD]).astype(BF16)
    val_new = qkv[:, QUARTER + HEAD :].astype(BF16)

    scale = HEAD ** (-0.5)
    l_mask.wait()
    queries = []
    start = []
    for request in range(2):
        span = slice(request * TREE, (request + 1) * TREE)
        q = jnp.concatenate([part[span] for part in heads_q], axis=0)
        allowed = jnp.concatenate([tree_mask[request]] * HEADS, axis=0) > 0
        scores = jnp.where(allowed, mm_nt(q, key_new[span]) * scale, -jnp.inf)
        peak = jnp.max(scores, axis=1, keepdims=True)
        weights = jnp.exp(scores - peak)
        queries.append(q)
        start.append(
            (
                peak,
                jnp.sum(weights, axis=1, keepdims=True),
                mm(weights.astype(BF16), val_new[span]),
            )
        )
    for copy in l_cache:
        copy.wait()

    def step(block, carry):
        found = []
        for request in range(2):
            peak, total, accum = carry[request]
            span = pl.ds(pl.multiple_of(block * BLOCK, BLOCK), BLOCK)
            limit = length0 if request == 0 else length1
            inside = block * BLOCK + iota((1, BLOCK), 1) < limit
            scores = mm_nt(queries[request], kbuf[request, span, :]) * scale
            scores = jnp.where(inside, scores, -jnp.inf)
            peak_now = jnp.maximum(peak, jnp.max(scores, axis=1, keepdims=True))
            weights = jnp.exp(scores - peak_now)
            fade = jnp.exp(peak - peak_now)
            total = total * fade + jnp.sum(weights, axis=1, keepdims=True)
            accum = accum * fade + mm(weights.astype(BF16), vbuf[request, span, :])
            found.append((peak_now, total, accum))
        return tuple(found)

    done = lax.fori_loop(0, LONGEST // BLOCK, step, tuple(start))
    mixed = [(accum / total).astype(BF16) for unused, total, accum in done]
    heads = jnp.concatenate(
        [
            jnp.concatenate([part[h * TREE : (h + 1) * TREE] for part in mixed], axis=0)
            for h in range(HEADS)
        ],
        axis=1,
    )

    pl.semaphore_wait(barrier, PEERS)

    def quarter(index):
        return pl.ds(pl.multiple_of(index * QUARTER, QUARTER), QUARTER)

    l_wo.wait()
    rs_copies = {}
    for dx in (2, 1, 3):
        peer = (x + dx) % NX
        rs_send[dx - 1] = mm(heads, w_output[:, quarter(peer)]).astype(BF16)
        rs_copies[dx] = pltpu.make_async_remote_copy(
            src_ref=rs_send.at[dx - 1],
            dst_ref=rs_recv.at[dx - 1],
            send_sem=rs_ssem.at[dx - 1],
            recv_sem=rs_rsem.at[dx - 1],
            device_id=(req, peer),
            device_id_type=MESH,
        )
        rs_copies[dx].start()
    attn_own = mm(heads, w_output[:, quarter(x)])

    ord_all[0] = jnp.where(iota((8, HEAD), 1) < KEEP, order_s[0], order_s[1])
    ord_copies = []
    for dz in range(1, NZ):
        copy = pltpu.make_async_remote_copy(
            src_ref=ord_all.at[0],
            dst_ref=ord_all.at[dz],
            send_sem=ord_ssem.at[dz - 1],
            recv_sem=ord_rsem.at[dz - 1],
            device_id=place((z + dz) % NZ, y, core),
            device_id_type=MESH,
        )
        copy.start()
        ord_copies.append(copy)

    l_ids.wait()
    ids_lane = jnp.concatenate([ids[0], ids[1]], axis=1)
    expert = iota((CHIPS, TOKENS), 0)
    picked = ids_lane[0:1, :] == expert
    for choice in range(1, 4):
        picked = picked | (ids_lane[choice : choice + 1, :] == expert)
    picked_f = jnp.where(picked, 1.0, 0.0)
    before = jnp.where(row < col, 1.0, 0.0).astype(BF16)
    slot = mm(picked_f.astype(BF16), before).astype(jnp.int32) - x * SHARE
    slot = jnp.where(picked, slot, -1)
    hit = slot[:, None, :] == iota((CHIPS, SHARE, TOKENS), 1)
    hit_f = jnp.where(hit, 1.0, 0.0)
    dmat[...] = hit_f.reshape(CHIPS * SHARE, TOKENS).astype(BF16)

    l_win.wait()
    part_rows = 64

    def split(index, unused):
        span = pl.ds(pl.multiple_of(index * part_rows, part_rows), part_rows)
        block = w_in_raw[span]
        w_in[0, span, :] = block[:, 0, :]
        w_in[1, span, :] = block[:, 1, :]
        return 0

    lax.fori_loop(0, WIDTH // part_rows // 2, split, 0)

    for dx in (1, 3, 2):
        rs_copies[dx].wait_recv()
    for dx in range(1, NX):
        attn_own = attn_own + rs_recv[dx - 1].astype(F32)
    ag_all[x] = attn_own.astype(BF16)
    ag_copies = {}
    for dx in (2, 1, 3):
        ag_copies[dx] = pltpu.make_async_remote_copy(
            src_ref=ag_all.at[x],
            dst_ref=ag_all.at[x],
            send_sem=ag_ssem.at[dx - 1],
            recv_sem=ag_rsem.at[dx - 1],
            device_id=(req, (x + dx) % NX),
            device_id_type=MESH,
        )
        ag_copies[dx].start()

    lax.fori_loop(WIDTH // part_rows // 2, WIDTH // part_rows, split, 0)
    l_gain2.wait()
    for dx in (1, 3, 2):
        wait_for(ag_all.at[(x + NX - dx) % NX], ag_rsem.at[dx - 1])

    resid = jnp.concatenate(
        [
            drafts[:, :, j * QUARTER : (j + 1) * QUARTER].reshape(TOKENS, QUARTER).astype(F32)
            + ag_all[j].astype(F32)
            for j in range(NX)
        ],
        axis=1,
    )
    mean2 = jnp.mean(resid * resid, axis=-1, keepdims=True)
    normed2[...] = (resid * lax.rsqrt(mean2 + EPSILON) * gain_moe[...]).astype(BF16)

    for half in range(2):
        found = mm(dmat[half * TOKENS : (half + 1) * TOKENS, :], normed2[...])
        send_buf[half * 16 : (half + 1) * 16] = found.reshape(16, SHARE, WIDTH).astype(BF16)
    where = {}
    for index, pair in enumerate(BATCHES):
        for side, dz in enumerate(pair):
            where[dz] = (index, side * NY)
    own_send = pltpu.make_async_copy(send_buf.at[chip], rows.at[0, 0, 0], disp_rsem.at[0])
    own_send.start()
    for dz in SEND_ORDER:
        for dy in range(NY):
            if dz == 0 and dy == 0:
                continue
            batch, base = where[dz]
            zz = (z + dz) % NZ
            yy = (y + dy) % NY
            pltpu.make_async_remote_copy(
                src_ref=send_buf.at[zz * NY + yy],
                dst_ref=rows.at[batch, 0, base + dy],
                send_sem=disp_ssem,
                recv_sem=disp_rsem.at[batch],
                device_id=place(zz, yy, core),
                device_id_type=MESH,
            ).start()

    l_router.wait()
    logits = mm_nt(w_router[...], normed2[...])
    chosen = jnp.where(picked, jax.nn.sigmoid(logits), 0.0)
    gates = (chosen / jnp.sum(chosen, axis=0, keepdims=True)).astype(BF16).astype(F32)
    comb[...] = jnp.where(hit, gates[:, None, :], 0.0).reshape(CHIPS * SHARE, TOKENS).astype(BF16)

    l_wout.wait()
    relays = {}
    siblings = {}

    def relay(batch):
        wait_for(rows.at[batch, 0], disp_rsem.at[batch])
        copy = pltpu.make_async_remote_copy(
            src_ref=rows.at[batch, 0],
            dst_ref=rows.at[batch, 1],
            send_sem=relay_ssem.at[batch],
            recv_sem=relay_rsem.at[batch],
            device_id=place(z, y, other),
            device_id_type=MESH,
        )
        copy.start()
        relays[batch] = copy

    def experts(batch):
        relays[batch].wait_recv()
        held = to_rows(rows[batch])
        gate = mm(held, w_in[0])
        upper = mm(held, w_in[1])
        act = (jnp.maximum(gate, 0.0) * upper).astype(BF16)
        part = mm(act, w_out[...]).astype(BF16)
        own_part[batch] = part[:TREE].astype(F32)
        sib_send[batch] = part[TREE:]
        copy = pltpu.make_async_remote_copy(
            src_ref=sib_send.at[batch],
            dst_ref=sib_recv.at[batch],
            send_sem=sib_ssem.at[batch],
            recv_sem=sib_rsem.at[batch],
            device_id=place(z, y, other),
            device_id_type=MESH,
        )
        copy.start()
        siblings[batch] = copy

    def give_back(batch):
        siblings[batch].wait_recv()
        total = own_part[batch] + sib_recv[batch].astype(F32)
        ret_send[batch] = total.reshape(8, SHARE, WIDTH).astype(BF16)
        for side, dz in enumerate(BATCHES[batch]):
            for dy in range(NY):
                source = ret_send.at[batch, side * NY + dy]
                if dz == 0 and dy == 0:
                    pltpu.make_async_copy(source, ret.at[chip], ret_rsem).start()
                    continue
                pltpu.make_async_remote_copy(
                    src_ref=source,
                    dst_ref=ret.at[chip],
                    send_sem=ret_ssem,
                    recv_sem=ret_rsem,
                    device_id=place((z + NZ - dz) % NZ, (y + NY - dy) % NY, core),
                    device_id_type=MESH,
                ).start()

    turn = (1, 2, 3, 0)
    for position, batch in enumerate(turn):
        relay(batch)
        if position:
            give_back(turn[position - 1])
        experts(batch)
    give_back(turn[-1])

    wait_for(ret, ret_rsem)
    mix_copies = {}

    def mixture(index):
        return mm_tn(comb[...], to_rows(ret[:, :, quarter(index)]))

    for dx in (2, 1, 3):
        peer = (x + dx) % NX
        mix_send[dx - 1] = mixture(peer).astype(BF16)
        mix_copies[dx] = pltpu.make_async_remote_copy(
            src_ref=mix_send.at[dx - 1],
            dst_ref=mix_recv.at[dx - 1],
            send_sem=mix_ssem.at[dx - 1],
            recv_sem=mix_rsem.at[dx - 1],
            device_id=(req, peer),
            device_id_type=MESH,
        )
        mix_copies[dx].start()
    total = mixture(x)
    total = total + drafts[:, :, quarter(x)].reshape(TOKENS, QUARTER).astype(F32)
    total = total + ag_all[x].astype(F32)
    l_slots.wait()
    slots_two = jnp.concatenate([slots[...], slots[...]], axis=1)
    slots_lane = jnp.where(iota((1, TOKENS), 1) < TREE, slots_two[0:1, :], slots_two[1:2, :])
    pick_row = iota((2 * KEEP, TOKENS), 0)
    pick_col = iota((2 * KEEP, TOKENS), 1)
    selector = jnp.where(
        (pick_row // KEEP == pick_col // TREE) & (pick_row % KEEP == slots_lane), 1.0, 0.0
    ).astype(BF16)
    for dx in (1, 3, 2):
        mix_copies[dx].wait_recv()
    for dx in range(1, NX):
        total = total + mix_recv[dx - 1].astype(F32)
    tree_out = total.astype(BF16)
    tree_out_ref[...] = tree_out.reshape(2, TREE, QUARTER)

    z_all[0] = mm(selector, tree_out).astype(BF16)
    z_copies = []
    for dz in (4, 3, 5, 2, 6, 1, 7):
        copy = pltpu.make_async_remote_copy(
            src_ref=z_all.at[0],
            dst_ref=z_all.at[dz],
            send_sem=z_ssem.at[dz - 1],
            recv_sem=z_rsem.at[dz - 1],
            device_id=place((z + dz) % NZ, y, core),
            device_id_type=MESH,
        )
        copy.start()
        z_copies.append(copy)
    for copy in ord_copies:
        copy.wait_recv()
    out_row = iota((256, 2 * KEEP), 0)
    out_col = iota((256, 2 * KEEP), 1)
    same = out_row % KEEP == out_col % KEEP
    target = z * KEEP + out_row // KEEP
    for copy in z_copies:
        copy.wait_recv()
    posted = jnp.zeros((256, QUARTER), F32)
    for dz in range(NZ):
        hits = same & (ord_all[dz][0:1, 0 : 2 * KEEP] == target)
        posted = posted + mm(jnp.where(hits, 1.0, 0.0).astype(BF16), z_all[dz])
    yc_send[...] = posted.reshape(8, 2 * KEEP, QUARTER).astype(BF16)
    yc_copies = []
    for dy in (2, 1, 3, 0):
        for flip in range(2):
            yy = (y + dy) % NY
            cc = other if flip else core
            index = yy * 2 + cc
            if dy == 0 and flip == 0:
                continue
            copy = pltpu.make_async_remote_copy(
                src_ref=yc_send.at[index],
                dst_ref=yc_recv.at[dy * 2 + flip],
                send_sem=yc_ssem.at[dy * 2 + flip - 1],
                recv_sem=yc_rsem.at[dy * 2 + flip - 1],
                device_id=place(z, yy, cc),
                device_id_type=MESH,
            )
            copy.start()
            yc_copies.append(copy)
    kept = yc_send[y * 2 + core].astype(F32)

    for dx in range(1, NX):
        rs_copies[dx].wait_send()
        ag_copies[dx].wait_send()
        mix_copies[dx].wait_send()
    for copy in ord_copies + z_copies:
        copy.wait_send()
    wait_for(send_buf.at[pl.ds(0, CHIPS - 1)], disp_ssem)
    wait_for(ret.at[pl.ds(0, CHIPS - 1)], ret_ssem)
    for batch in range(4):
        relays[batch].wait_send()
        siblings[batch].wait_send()
    for copy in yc_copies:
        copy.wait()
    for index in range(1, 8):
        kept = kept + yc_recv[index].astype(F32)
    accepted_ref[...] = kept.astype(BF16).reshape(2, KEEP, QUARTER)


def on_device(
    drafts,
    gain_attn,
    w_query,
    key_value_weight,
    w_output,
    cache,
    lengths,
    tree_mask,
    depths,
    gain_moe,
    w_router,
    expert_ids,
    w_in,
    w_out,
    slots,
    order,
):
    any_space = pl.BlockSpec(memory_space=pl.ANY)
    scalars = pl.BlockSpec(memory_space=pltpu.SMEM)
    in_specs = [any_space] * 16
    in_specs[6] = scalars
    in_specs[15] = scalars
    vmem = pltpu.VMEM
    sem = pltpu.SemaphoreType.DMA
    i32 = jnp.int32
    scratch = [
        vmem((2, TREE, WIDTH), BF16),
        vmem((1, WIDTH), F32),
        vmem((WIDTH, 640), BF16),
        vmem((QUARTER, WIDTH), BF16),
        vmem((2, LONGEST, HEAD), BF16),
        vmem((2, LONGEST, HEAD), BF16),
        vmem((2, TREE, TREE), i32),
        vmem((2, TREE), i32),
        vmem((1, WIDTH), F32),
        vmem((CHIPS, WIDTH), BF16),
        vmem((2, 4, TREE), i32),
        vmem((WIDTH, 2, HALF_FF), BF16),
        vmem((2, WIDTH, HALF_FF), BF16),
        vmem((HALF_FF, WIDTH), BF16),
        vmem((2, TREE), i32),
        sem((20,)),
        vmem((3, TOKENS, QUARTER), BF16),
        vmem((3, TOKENS, QUARTER), BF16),
        sem((3,)),
        sem((3,)),
        vmem((4, TOKENS, QUARTER), BF16),
        sem((3,)),
        sem((3,)),
        vmem((256, TOKENS), BF16),
        vmem((256, TOKENS), BF16),
        vmem((TOKENS, WIDTH), BF16),
        vmem((CHIPS, SHARE, WIDTH), BF16),
        vmem((4, 2, 8, SHARE, WIDTH), BF16),
        vmem((4, TREE, WIDTH), F32),
        vmem((4, TREE, WIDTH), BF16),
        vmem((4, TREE, WIDTH), BF16),
        vmem((4, 8, SHARE, WIDTH), BF16),
        vmem((CHIPS, SHARE, WIDTH), BF16),
        sem,
        sem((4,)),
        sem((4,)),
        sem((4,)),
        sem((4,)),
        sem((4,)),
        sem,
        sem,
        vmem((3, TOKENS, QUARTER), BF16),
        vmem((3, TOKENS, QUARTER), BF16),
        sem((3,)),
        sem((3,)),
        vmem((NZ, 8, HEAD), i32),
        sem((7,)),
        sem((7,)),
        vmem((NZ, 2 * KEEP, QUARTER), BF16),
        sem((7,)),
        sem((7,)),
        vmem((8, 2 * KEEP, QUARTER), BF16),
        vmem((8, 2 * KEEP, QUARTER), BF16),
        sem((7,)),
        sem((7,)),
    ]
    return pl.pallas_call(
        layer,
        out_shape=(
            jax.ShapeDtypeStruct((2, TREE, QUARTER), BF16),
            jax.ShapeDtypeStruct((2, KEEP, QUARTER), BF16),
        ),
        in_specs=in_specs,
        out_specs=(pl.BlockSpec(memory_space=vmem), pl.BlockSpec(memory_space=vmem)),
        scratch_shapes=scratch,
        compiler_params=pltpu.CompilerParams(
            collective_id=0, has_side_effects=True, vmem_limit_bytes=56 * 1024 * 1024
        ),
    )(
        drafts,
        gain_attn.reshape(1, WIDTH),
        w_query,
        key_value_weight,
        w_output,
        cache,
        lengths,
        tree_mask,
        depths,
        gain_moe.reshape(1, WIDTH),
        w_router.T,
        expert_ids.transpose(0, 2, 1),
        w_in.reshape(WIDTH, 2, HALF_FF),
        w_out.reshape(HALF_FF, WIDTH),
        slots,
        order,
    )


def solution(mesh):
    placed = (
        P("req", None, None),
        P(),
        P(None, "tp"),
        P(),
        P("tp", None),
        P("req", None, None, None, None),
        P("req"),
        P("req", None, None),
        P("req", None),
        P(),
        P(),
        P("req", None, None),
        P("req", None, None, None),
        P("req", None, None),
        P("req", None),
        P("req"),
    )
    return jax.shard_map(
        on_device,
        mesh=mesh,
        in_specs=placed,
        out_specs=(P("req", None, "tp"), P("req", None, "tp")),
        check_vma=False,
    )
```

```python
import jax
import jax.numpy as jnp
from jax import lax
from jax.experimental import pallas as pl
from jax.experimental.pallas import tpu as pltpu
from jax.sharding import PartitionSpec as P

KEEP = 16
EPSILON = 1e-06
THETA = 1000000.0
NX = 4
NY = 4
NZ = 8
CHIPS = 32
SHARE = 8
HEAD = 128
HEADS = 3
TREE = 64
TOKENS = 128
WIDTH = 1536
QUARTER = 384
LONGEST = 3072
BLOCK = 1024
HALF_FF = 384
PEERS = 38
BATCHES = ((0, 4), (1, 7), (2, 6), (3, 5))
SEND_ORDER = (1, 7, 2, 6, 3, 5, 4, 0)
F32 = jnp.float32
BF16 = jnp.bfloat16
MESH = pl.DeviceIdType.MESH


def mm(left, right):
    return jnp.dot(left, right, preferred_element_type=F32)


def mm_nt(left, right):
    return lax.dot_general(left, right, (((1,), (1,)), ((), ())), preferred_element_type=F32)


def mm_tn(left, right):
    return lax.dot_general(left, right, (((0,), (0,)), ((), ())), preferred_element_type=F32)


def iota(shape, dim):
    return lax.broadcasted_iota(jnp.int32, shape, dim)


def to_rows(blocks):
    shape = blocks.shape
    rows = 1
    for size in shape[:-1]:
        rows *= size
    return blocks.astype(F32).reshape(rows, shape[-1]).astype(BF16)


def wait_for(ref, sem):
    pltpu.make_async_copy(ref, ref, sem).wait()


def layer(
    drafts_h,
    gain_attn_h,
    w_query_h,
    kv_weight_h,
    w_output_h,
    cache_h,
    lengths_s,
    tree_mask_h,
    depths_h,
    gain_moe_h,
    w_router_h,
    ids_h,
    w_in_h,
    w_out_h,
    slots_h,
    order_s,
    tree_out_ref,
    accepted_ref,
    drafts,
    gain_attn,
    w_qkv,
    w_output,
    kbuf,
    vbuf,
    tree_mask,
    depths,
    gain_moe,
    w_router,
    ids,
    w_in_raw,
    w_in,
    w_out,
    slots,
    load_sem,
    rs_send,
    rs_recv,
    rs_ssem,
    rs_rsem,
    score_buf,
    stat_all,
    stat_ssem,
    stat_rsem,
    logit_all,
    logit_ssem,
    logit_rsem,
    dmat,
    comb,
    send_buf,
    landed,
    rows,
    xa_ssem,
    xa_rsem,
    ret_x,
    xb_ssem,
    xb_rsem,
    own_part,
    sib_send,
    sib_recv,
    ret_send,
    ret,
    disp_ssem,
    disp_rsem,
    relay_ssem,
    relay_rsem,
    sib_ssem,
    sib_rsem,
    ret_ssem,
    ret_rsem,
    route,
    ord_all,
    ord_ssem,
    ord_rsem,
    z_all,
    z_ssem,
    z_rsem,
    yc_send,
    yc_recv,
    yc_ssem,
    yc_rsem,
):
    x = lax.axis_index("tp")
    req = lax.axis_index("req")
    core = req % 2
    chip = req // 2
    y = chip % NY
    z = chip // NY
    kv_head = x // 2
    other = 1 - core

    def place(zz, yy, cc):
        return ((zz * NY + yy) * 2 + cc, x)

    barrier = pltpu.get_barrier_semaphore()

    def greet(device):
        pl.semaphore_signal(barrier, inc=1, device_id=device, device_id_type=MESH)

    for dx in range(1, NX):
        greet((req, (x + dx) % NX))
    for dz in range(NZ):
        for dy in range(NY):
            if dz or dy:
                greet(place((z + dz) % NZ, (y + dy) % NY, core))
    for dy in range(NY):
        greet(place(z, (y + dy) % NY, other))

    loads = []

    def load(source, target):
        copy = pltpu.make_async_copy(source, target, load_sem.at[len(loads)])
        copy.start()
        loads.append(copy)
        return copy

    l_drafts = load(drafts_h, drafts)
    l_gain = load(gain_attn_h, gain_attn)
    l_depths = load(depths_h, depths)
    l_wq = load(w_query_h, w_qkv.at[:, pl.ds(0, QUARTER)])
    l_wk = load(
        kv_weight_h.at[:, pl.ds(pl.multiple_of(kv_head * HEAD, HEAD), HEAD)],
        w_qkv.at[:, pl.ds(QUARTER, HEAD)],
    )
    l_wv = load(
        kv_weight_h.at[:, pl.ds(pl.multiple_of(256 + kv_head * HEAD, HEAD), HEAD)],
        w_qkv.at[:, pl.ds(QUARTER + HEAD, HEAD)],
    )
    l_mask = load(tree_mask_h, tree_mask)
    l_cache = []
    for request in range(2):
        l_cache.append(load(cache_h.at[request, 0, kv_head], kbuf.at[request]))
        l_cache.append(load(cache_h.at[request, 1, kv_head], vbuf.at[request]))
    l_depths.wait()
    length0 = lengths_s[0]
    length1 = lengths_s[1]
    row = iota((TOKENS, TOKENS), 0)
    col = iota((TOKENS, TOKENS), 1)
    spread = jnp.concatenate([depths[...], depths[...]], axis=1)
    pos_lane = jnp.where(
        iota((1, TOKENS), 1) < TREE, spread[0:1, :] + length0, spread[1:2, :] + length1
    ).astype(F32)
    positions = jnp.sum(jnp.where(row == col, pos_lane, 0.0), axis=1, keepdims=True)
    lane = iota((1, HEAD), 1) % (HEAD // 2)
    freqs = jnp.exp(-jnp.log(jnp.float32(THETA)) * lane.astype(F32) / (HEAD // 2))
    angles = positions * freqs
    cosine = jnp.cos(angles)
    sine = jnp.sin(angles)
    sine = jnp.where(col < HEAD // 2, -sine, sine)

    def rotary(values):
        return values * cosine + pltpu.roll(values, HEAD // 2, 1) * sine

    l_drafts.wait()
    l_gain.wait()
    inputs = drafts[...].reshape(TOKENS, WIDTH).astype(F32)
    mean = jnp.mean(inputs * inputs, axis=-1, keepdims=True)
    normed = (inputs * lax.rsqrt(mean + EPSILON) * gain_attn[...]).astype(BF16)
    l_wq.wait()
    l_wk.wait()
    l_wv.wait()
    qkv = mm(normed, w_qkv[...])
    heads_q = [
        rotary(qkv[:, h * HEAD : (h + 1) * HEAD]).astype(BF16) for h in range(HEADS)
    ]
    key_new = rotary(qkv[:, QUARTER : QUARTER + HEAD]).astype(BF16)
    val_new = qkv[:, QUARTER + HEAD :].astype(BF16)

    l_wo = load(w_output_h, w_output)
    l_ids = load(ids_h, ids)
    l_win = load(w_in_h, w_in_raw)
    l_gain2 = load(gain_moe_h, gain_moe)
    l_router = load(w_router_h, w_router)
    l_slots = load(slots_h, slots)
    l_wout = load(w_out_h, w_out)

    scale = HEAD ** (-0.5)
    l_mask.wait()

    def quarter(index):
        return pl.ds(pl.multiple_of(index * QUARTER, QUARTER), QUARTER)

    def lanes_max(values):
        found = values[:, :HEAD]
        for index in range(1, values.shape[1] // HEAD):
            found = jnp.maximum(found, values[:, index * HEAD : (index + 1) * HEAD])
        return found

    def lanes_sum(values):
        found = values[:, :HEAD]
        for index in range(1, values.shape[1] // HEAD):
            found = found + values[:, index * HEAD : (index + 1) * HEAD]
        return found

    def attend(request, limit):
        own = slice(request * TREE, (request + 1) * TREE)
        q = jnp.concatenate([part[own] for part in heads_q], axis=0)
        allowed = jnp.concatenate([tree_mask[request]] * HEADS, axis=0) > 0
        tree_scores = jnp.where(allowed, mm_nt(q, key_new[own]), -jnp.inf)
        l_cache[2 * request].wait()

        def score(block, running):
            span = pl.ds(pl.multiple_of(block * BLOCK, BLOCK), BLOCK)
            inside = block * BLOCK + iota((1, BLOCK), 1) < limit
            scores = jnp.where(inside, mm_nt(q, kbuf[request, span, :]), -jnp.inf)
            score_buf[:, span] = scores
            return jnp.maximum(running, lanes_max(scores))

        running = lax.fori_loop(
            0, LONGEST // BLOCK, score, jnp.full((HEADS * TREE, HEAD), -jnp.inf, F32)
        )
        peak = jnp.maximum(
            jnp.max(running, axis=1, keepdims=True), jnp.max(tree_scores, axis=1, keepdims=True)
        )
        tree_weights = jnp.exp((tree_scores - peak) * scale)
        accum = mm(tree_weights.astype(BF16), val_new[own])
        l_cache[2 * request + 1].wait()

        def collect(block, carry):
            total, accum = carry
            span = pl.ds(pl.multiple_of(block * BLOCK, BLOCK), BLOCK)
            weights = jnp.exp((score_buf[:, span] - peak) * scale)
            accum = accum + mm(weights.astype(BF16), vbuf[request, span, :])
            return total + lanes_sum(weights), accum

        total, accum = lax.fori_loop(
            0, LONGEST // BLOCK, collect, (jnp.zeros((HEADS * TREE, HEAD), F32), accum)
        )
        total = jnp.sum(total, axis=1, keepdims=True) + jnp.sum(
            tree_weights, axis=1, keepdims=True
        )
        mixed = (accum / total).astype(BF16)
        return jnp.concatenate(
            [mixed[h * TREE : (h + 1) * TREE] for h in range(HEADS)], axis=1
        )

    rs_copies = {}
    owns = []

    def project(request, heads):
        for dx in (2, 1, 3):
            peer = (x + dx) % NX
            rs_send[dx - 1, request] = mm(heads, w_output[:, quarter(peer)]).astype(BF16)
            copy = pltpu.make_async_remote_copy(
                src_ref=rs_send.at[dx - 1, request],
                dst_ref=rs_recv.at[dx - 1, request],
                send_sem=rs_ssem.at[dx - 1, request],
                recv_sem=rs_rsem.at[dx - 1, request],
                device_id=(req, peer),
                device_id_type=MESH,
            )
            copy.start()
            rs_copies[dx, request] = copy
        owns.append(mm(heads, w_output[:, quarter(x)]))

    heads0 = attend(0, length0)
    pl.semaphore_wait(barrier, PEERS)
    l_wo.wait()
    project(0, heads0)
    project(1, attend(1, length1))

    ord_all[0] = jnp.where(iota((8, HEAD), 1) < KEEP, order_s[0], order_s[1])
    ord_copies = []
    for dz in range(1, NZ):
        copy = pltpu.make_async_remote_copy(
            src_ref=ord_all.at[0],
            dst_ref=ord_all.at[dz],
            send_sem=ord_ssem.at[dz - 1],
            recv_sem=ord_rsem.at[dz - 1],
            device_id=place((z + dz) % NZ, y, core),
            device_id_type=MESH,
        )
        copy.start()
        ord_copies.append(copy)

    l_ids.wait()
    ids_lane = jnp.concatenate([ids[0], ids[1]], axis=1)
    expert = iota((CHIPS, TOKENS), 0)
    picked = ids_lane[0:1, :] == expert
    for choice in range(1, 4):
        picked = picked | (ids_lane[choice : choice + 1, :] == expert)
    picked_f = jnp.where(picked, 1.0, 0.0)
    before = jnp.where(row < col, 1.0, 0.0).astype(BF16)
    slot = mm(picked_f.astype(BF16), before).astype(jnp.int32)
    slot = jnp.where(picked, slot, -1)
    hit = slot[:, None, :] == iota((CHIPS, NX * SHARE, TOKENS), 1)
    hit_f = jnp.where(hit, 1.0, 0.0)
    dmat[...] = hit_f.reshape(CHIPS * NX * SHARE, TOKENS).astype(BF16)

    l_win.wait()
    part_rows = 64

    def split(index, unused):
        span = pl.ds(pl.multiple_of(index * part_rows, part_rows), part_rows)
        block = w_in_raw[span]
        w_in[0, span, :] = block[:, 0, :]
        w_in[1, span, :] = block[:, 1, :]
        return 0

    lax.fori_loop(0, WIDTH // part_rows, split, 0)
    l_gain2.wait()

    resid = []
    for request in range(2):
        for dx in (1, 3, 2):
            rs_copies[dx, request].wait_recv()
        found = owns[request] + drafts[request, :, quarter(x)].astype(F32)
        for dx in range(1, NX):
            found = found + rs_recv[dx - 1, request].astype(F32)
        resid.append(found)
    resid = jnp.concatenate(resid, axis=0)
    squares = jnp.sum(resid * resid, axis=1, keepdims=True)
    stat = jnp.sum(jnp.where(row == col, squares, 0.0), axis=0, keepdims=True)
    stat_all[0] = jnp.broadcast_to(stat, (8, TOKENS))
    stat_copies = []
    for dx in (2, 1, 3):
        copy = pltpu.make_async_remote_copy(
            src_ref=stat_all.at[0],
            dst_ref=stat_all.at[dx],
            send_sem=stat_ssem.at[dx - 1],
            recv_sem=stat_rsem.at[dx - 1],
            device_id=(req, (x + dx) % NX),
            device_id_type=MESH,
        )
        copy.start()
        stat_copies.append(copy)
    scaled = resid * gain_moe[:, quarter(x)]
    for copy in stat_copies:
        copy.wait_recv()
    for dx in range(1, NX):
        stat = stat + stat_all[dx][0:1, :]
    squares = jnp.sum(jnp.where(row == col, stat, 0.0), axis=1, keepdims=True)
    normed2 = (scaled * lax.rsqrt(squares / WIDTH + EPSILON)).astype(BF16)

    for half in range(2):
        found = mm(dmat[half * 512 : (half + 1) * 512, :], normed2)
        send_buf[half * 16 : (half + 1) * 16] = found.reshape(16, NX, SHARE, QUARTER).astype(BF16)
    where = {}
    for index, pair in enumerate(BATCHES):
        for side, dz in enumerate(pair):
            where[dz] = (index, side * NY)
    own_send = pltpu.make_async_copy(send_buf.at[chip], landed.at[0, 0], disp_rsem.at[0])
    own_send.start()
    for dz in SEND_ORDER:
        for dy in range(NY):
            if dz == 0 and dy == 0:
                continue
            batch, base = where[dz]
            zz = (z + dz) % NZ
            yy = (y + dy) % NY
            pltpu.make_async_remote_copy(
                src_ref=send_buf.at[zz * NY + yy],
                dst_ref=landed.at[batch, base + dy],
                send_sem=disp_ssem,
                recv_sem=disp_rsem.at[batch],
                device_id=place(zz, yy, core),
                device_id_type=MESH,
            ).start()

    l_router.wait()
    logit_all[0] = mm_nt(w_router[:, quarter(x)], normed2)
    logit_copies = []
    for dx in (2, 1, 3):
        copy = pltpu.make_async_remote_copy(
            src_ref=logit_all.at[0],
            dst_ref=logit_all.at[dx],
            send_sem=logit_ssem.at[dx - 1],
            recv_sem=logit_rsem.at[dx - 1],
            device_id=(req, (x + dx) % NX),
            device_id_type=MESH,
        )
        copy.start()
        logit_copies.append(copy)
    for copy in logit_copies:
        copy.wait_recv()
    logits = (logit_all[0] + logit_all[1]) + (logit_all[2] + logit_all[3])
    chosen = jnp.where(picked, jax.nn.sigmoid(logits), 0.0)
    gates = (chosen / jnp.sum(chosen, axis=0, keepdims=True)).astype(BF16).astype(F32)
    weighed = jnp.where(hit, gates[:, None, :], 0.0).reshape(CHIPS * NX * SHARE, TOKENS)
    comb[...] = weighed.T.astype(BF16)

    l_wout.wait()
    relays = {}
    siblings = {}

    def to_planes(batch):
        wait_for(landed.at[batch], disp_rsem.at[batch])
        pltpu.make_async_copy(
            landed.at[batch, :, x], rows.at[batch, 0, x], xa_rsem.at[batch]
        ).start()
        for dx in (2, 1, 3):
            peer = (x + dx) % NX
            pltpu.make_async_remote_copy(
                src_ref=landed.at[batch, :, peer],
                dst_ref=rows.at[batch, 0, x],
                send_sem=xa_ssem.at[batch],
                recv_sem=xa_rsem.at[batch],
                device_id=(req, peer),
                device_id_type=MESH,
            ).start()

    def relay(batch):
        wait_for(rows.at[batch, 0], xa_rsem.at[batch])
        copy = pltpu.make_async_remote_copy(
            src_ref=rows.at[batch, 0],
            dst_ref=rows.at[batch, 1],
            send_sem=relay_ssem.at[batch],
            recv_sem=relay_rsem.at[batch],
            device_id=place(z, y, other),
            device_id_type=MESH,
        )
        copy.start()
        relays[batch] = copy

    def experts(batch):
        relays[batch].wait_recv()
        held = jnp.concatenate([to_rows(rows[batch, :, part]) for part in range(NX)], axis=1)
        gate = mm(held, w_in[0])
        upper = mm(held, w_in[1])
        act = (jnp.maximum(gate, 0.0) * upper).astype(BF16)
        part = mm(act, w_out[...]).astype(BF16)
        own_part[batch] = part[:TREE].astype(F32)
        sib_send[batch] = part[TREE:]
        copy = pltpu.make_async_remote_copy(
            src_ref=sib_send.at[batch],
            dst_ref=sib_recv.at[batch],
            send_sem=sib_ssem.at[batch],
            recv_sem=sib_rsem.at[batch],
            device_id=place(z, y, other),
            device_id_type=MESH,
        )
        copy.start()
        siblings[batch] = copy

    def from_planes(batch):
        siblings[batch].wait_recv()
        total = own_part[batch] + sib_recv[batch].astype(F32)
        for part in range(NX):
            ret_x[batch, part] = (
                total[:, part * QUARTER : (part + 1) * QUARTER]
                .reshape(8, SHARE, QUARTER)
                .astype(BF16)
            )
        pltpu.make_async_copy(
            ret_x.at[batch, x], ret_send.at[batch, :, x], xb_rsem.at[batch]
        ).start()
        for dx in (2, 1, 3):
            peer = (x + dx) % NX
            pltpu.make_async_remote_copy(
                src_ref=ret_x.at[batch, peer],
                dst_ref=ret_send.at[batch, :, x],
                send_sem=xb_ssem.at[batch],
                recv_sem=xb_rsem.at[batch],
                device_id=(req, peer),
                device_id_type=MESH,
            ).start()

    def give_back(batch):
        wait_for(ret_send.at[batch], xb_rsem.at[batch])
        for side, dz in enumerate(BATCHES[batch]):
            for dy in range(NY):
                source = ret_send.at[batch, side * NY + dy]
                if dz == 0 and dy == 0:
                    pltpu.make_async_copy(source, ret.at[chip], ret_rsem).start()
                    continue
                pltpu.make_async_remote_copy(
                    src_ref=source,
                    dst_ref=ret.at[chip],
                    send_sem=ret_ssem,
                    recv_sem=ret_rsem,
                    device_id=place((z + NZ - dz) % NZ, (y + NY - dy) % NY, core),
                    device_id_type=MESH,
                ).start()

    first, second, third, fourth = 1, 2, 3, 0
    to_planes(first)
    relay(first)
    to_planes(second)
    experts(first)
    from_planes(first)
    relay(second)
    to_planes(third)
    experts(second)
    give_back(first)
    from_planes(second)
    relay(third)
    to_planes(fourth)
    experts(third)
    give_back(second)
    from_planes(third)
    relay(fourth)
    experts(fourth)
    give_back(third)
    from_planes(fourth)
    give_back(fourth)

    l_slots.wait()
    slots_two = jnp.concatenate([slots[...], slots[...]], axis=1)
    slots_lane = jnp.where(iota((1, TOKENS), 1) < TREE, slots_two[0:1, :], slots_two[1:2, :])
    pick_row = iota((2 * KEEP, TOKENS), 0)
    pick_col = iota((2 * KEEP, TOKENS), 1)
    selector = jnp.where(
        (pick_row // KEEP == pick_col // TREE) & (pick_row % KEEP == slots_lane), 1.0, 0.0
    ).astype(BF16)
    for copy in ord_copies:
        copy.wait_recv()
    out_row = iota((256, 2 * KEEP), 0)
    out_col = iota((256, 2 * KEEP), 1)
    same = out_row % KEEP == out_col % KEEP
    target = z * KEEP + out_row // KEEP
    hits = [
        jnp.where(same & (ord_all[dz][0:1, 0 : 2 * KEEP] == target), 1.0, 0.0)
        for dz in range(NZ)
    ]
    route[...] = jnp.concatenate(hits, axis=1).astype(BF16)

    wait_for(ret, ret_rsem)
    tree_out = (resid + mm(comb[...], to_rows(ret[...]))).astype(BF16)
    tree_out_ref[...] = tree_out.reshape(2, TREE, QUARTER)

    z_all[0] = mm(selector, tree_out).astype(BF16)
    z_copies = []
    for dz in (4, 3, 5, 2, 6, 1, 7):
        copy = pltpu.make_async_remote_copy(
            src_ref=z_all.at[0],
            dst_ref=z_all.at[dz],
            send_sem=z_ssem.at[dz - 1],
            recv_sem=z_rsem.at[dz - 1],
            device_id=place((z + dz) % NZ, y, core),
            device_id_type=MESH,
        )
        copy.start()
        z_copies.append(copy)
    for copy in z_copies:
        copy.wait_recv()
    posted = mm(route[...], z_all[...].reshape(256, QUARTER))
    yc_send[...] = posted.reshape(8, 2 * KEEP, QUARTER).astype(BF16)
    yc_copies = []
    for dy in (2, 1, 3, 0):
        for flip in range(2):
            yy = (y + dy) % NY
            cc = other if flip else core
            index = yy * 2 + cc
            if dy == 0 and flip == 0:
                continue
            copy = pltpu.make_async_remote_copy(
                src_ref=yc_send.at[index],
                dst_ref=yc_recv.at[dy * 2 + flip],
                send_sem=yc_ssem.at[dy * 2 + flip - 1],
                recv_sem=yc_rsem.at[dy * 2 + flip - 1],
                device_id=place(z, yy, cc),
                device_id_type=MESH,
            )
            copy.start()
            yc_copies.append(copy)
    kept = yc_send[y * 2 + core].astype(F32)

    for copy in list(rs_copies.values()) + stat_copies + logit_copies + ord_copies + z_copies:
        copy.wait_send()
    wait_for(send_buf.at[pl.ds(0, CHIPS - 1)], disp_ssem)
    wait_for(ret.at[pl.ds(0, CHIPS - 1)], ret_ssem)
    for batch in range(4):
        relays[batch].wait_send()
        siblings[batch].wait_send()
        wait_for(rows.at[batch, 0, pl.ds(0, NX - 1)], xa_ssem.at[batch])
        wait_for(ret_x.at[batch, pl.ds(0, NX - 1)], xb_ssem.at[batch])
    for copy in yc_copies:
        copy.wait()
    for index in range(1, 8):
        kept = kept + yc_recv[index].astype(F32)
    accepted_ref[...] = kept.astype(BF16).reshape(2, KEEP, QUARTER)


def on_device(
    drafts,
    gain_attn,
    w_query,
    key_value_weight,
    w_output,
    cache,
    lengths,
    tree_mask,
    depths,
    gain_moe,
    w_router,
    expert_ids,
    w_in,
    w_out,
    slots,
    order,
):
    any_space = pl.BlockSpec(memory_space=pl.ANY)
    scalars = pl.BlockSpec(memory_space=pltpu.SMEM)
    in_specs = [any_space] * 16
    in_specs[6] = scalars
    in_specs[15] = scalars
    vmem = pltpu.VMEM
    sem = pltpu.SemaphoreType.DMA
    i32 = jnp.int32
    scratch = [
        vmem((2, TREE, WIDTH), BF16),
        vmem((1, WIDTH), F32),
        vmem((WIDTH, 640), BF16),
        vmem((QUARTER, WIDTH), BF16),
        vmem((2, LONGEST, HEAD), BF16),
        vmem((2, LONGEST, HEAD), BF16),
        vmem((2, TREE, TREE), i32),
        vmem((2, TREE), i32),
        vmem((1, WIDTH), F32),
        vmem((CHIPS, WIDTH), BF16),
        vmem((2, 4, TREE), i32),
        vmem((WIDTH, 2, HALF_FF), BF16),
        vmem((2, WIDTH, HALF_FF), BF16),
        vmem((HALF_FF, WIDTH), BF16),
        vmem((2, TREE), i32),
        sem((20,)),
        vmem((3, 2, TREE, QUARTER), BF16),
        vmem((3, 2, TREE, QUARTER), BF16),
        sem((3, 2)),
        sem((3, 2)),
        vmem((HEADS * TREE, LONGEST), F32),
        vmem((NX, 8, TOKENS), F32),
        sem((3,)),
        sem((3,)),
        vmem((NX, CHIPS, TOKENS), F32),
        sem((3,)),
        sem((3,)),
        vmem((CHIPS * NX * SHARE, TOKENS), BF16),
        vmem((TOKENS, CHIPS * NX * SHARE), BF16),
        vmem((CHIPS, NX, SHARE, QUARTER), BF16),
        vmem((4, 8, NX, SHARE, QUARTER), BF16),
        vmem((4, 2, NX, 8, SHARE, QUARTER), BF16),
        sem((4,)),
        sem((4,)),
        vmem((4, NX, 8, SHARE, QUARTER), BF16),
        sem((4,)),
        sem((4,)),
        vmem((4, TREE, WIDTH), F32),
        vmem((4, TREE, WIDTH), BF16),
        vmem((4, TREE, WIDTH), BF16),
        vmem((4, 8, NX, SHARE, QUARTER), BF16),
        vmem((CHIPS, NX, SHARE, QUARTER), BF16),
        sem,
        sem((4,)),
        sem((4,)),
        sem((4,)),
        sem((4,)),
        sem((4,)),
        sem,
        sem,
        vmem((256, 256), BF16),
        vmem((NZ, 8, HEAD), i32),
        sem((7,)),
        sem((7,)),
        vmem((NZ, 2 * KEEP, QUARTER), BF16),
        sem((7,)),
        sem((7,)),
        vmem((8, 2 * KEEP, QUARTER), BF16),
        vmem((8, 2 * KEEP, QUARTER), BF16),
        sem((7,)),
        sem((7,)),
    ]
    return pl.pallas_call(
        layer,
        out_shape=(
            jax.ShapeDtypeStruct((2, TREE, QUARTER), BF16),
            jax.ShapeDtypeStruct((2, KEEP, QUARTER), BF16),
        ),
        in_specs=in_specs,
        out_specs=(pl.BlockSpec(memory_space=vmem), pl.BlockSpec(memory_space=vmem)),
        scratch_shapes=scratch,
        compiler_params=pltpu.CompilerParams(
            collective_id=0, has_side_effects=True, vmem_limit_bytes=56 * 1024 * 1024
        ),
    )(
        drafts,
        gain_attn.reshape(1, WIDTH),
        w_query,
        key_value_weight,
        w_output,
        cache,
        lengths,
        tree_mask,
        depths,
        gain_moe.reshape(1, WIDTH),
        w_router.T,
        expert_ids.transpose(0, 2, 1),
        w_in.reshape(WIDTH, 2, HALF_FF),
        w_out.reshape(HALF_FF, WIDTH),
        slots,
        order,
    )


def solution(mesh):
    placed = (
        P("req", None, None),
        P(),
        P(None, "tp"),
        P(),
        P("tp", None),
        P("req", None, None, None, None),
        P("req"),
        P("req", None, None),
        P("req", None),
        P(),
        P(),
        P("req", None, None),
        P("req", None, None, None),
        P("req", None, None),
        P("req", None),
        P("req"),
    )
    return jax.shard_map(
        on_device,
        mesh=mesh,
        in_specs=placed,
        out_specs=(P("req", None, "tp"), P("req", None, "tp")),
        check_vma=False,
    )
```
